32 devices in a mesh: dp: 8 (over y, x, core), vocab: 4 (over z).
Axes of the slice: x: 2, y: 2, z: 4, core: 2. Of those that a mesh axis runs over, the one named last changes fastest.
Arguments:
- hidden_current: bfloat16 [256, 4096], P(('dp', 'vocab'))
- hidden_proximal: bfloat16 [256, 4096], P(('dp', 'vocab'))
- head_current: bfloat16 [4096, 128256], P(None, ('dp', 'vocab'))
- head_proximal: bfloat16 [4096, 128256], P(None, ('dp', 'vocab'))
- targets: int32 [256], P(('dp', 'vocab')), may hold values from 0 to 128255
- loss_mask: int32 [256], P(('dp', 'vocab')), may hold values from 0 to 1, as said below
- lengths: int32 [32], P(('dp', 'vocab')), may hold values from 1 to 8
- behavior_logprob: float32 [256], P(('dp', 'vocab')), may hold values from -14 to -10
- advantages: float32 [256], P(('dp', 'vocab')), may hold values from -6 to 6
Outputs:
- token_loss: float32 [256], P(('dp', 'vocab'))
- current_logprob: float32 [256], P(('dp', 'vocab'))
- stats: float32 [3], replicated
The draws below stay inside these ranges and needn't reach their ends.
Inputs may be any that keep to these rules, and one draw needn't show every extreme that they name: `loss_mask`: 1 at the first position of every sequence's window.
All inputs are finite; a program needn't handle non-finite values.
Results may differ from the reference program's by a relative error of at most 0.0003.
Values may be sent and summed in bfloat16 or wider, within the bound.
A program may use at most 128 MiB of HBM per device.

```python
import math
import jax
import jax.numpy as jnp
import numpy as np
from jax import lax

D = 4096
VOCAB = 128256
POSITIONS = 8
SEQS = 32
TOKENS = 256


def hidden_base(key):
    return jax.random.normal(jax.random.fold_in(key, 21), (TOKENS, D), jnp.float32)


def head_base(key):
    return jax.random.normal(jax.random.fold_in(key, 41), (D, VOCAB), jnp.float32) * D ** (-0.5)


def draw_hidden_current(key, part):
    return hidden_base(key).astype(jnp.bfloat16)


def draw_hidden_proximal(key, part):
    noise = jax.random.normal(jax.random.fold_in(key, 22), (TOKENS, D), jnp.float32)
    return (hidden_base(key) + 0.15 * noise).astype(jnp.bfloat16)


def draw_head_current(key, part):
    return head_base(key).astype(jnp.bfloat16)


def draw_head_proximal(key, part):
    spread = 0.15
    noise = jax.random.normal(jax.random.fold_in(key, 42), (D, VOCAB), jnp.float32) * D ** (-0.5)
    return (head_base(key) + spread * noise).astype(jnp.bfloat16)


def draw_loss_mask(key, part):
    coin = jax.random.randint(jax.random.fold_in(key, 51), (TOKENS,), 0, 4)
    place = jnp.arange(TOKENS, dtype=jnp.int32) % POSITIONS
    return jnp.where((place == 0) | (coin < 3), 1, 0).astype(jnp.int32)


def touch_ends(values, key, low, high):
    longest = values.shape.index(max(values.shape))
    spots = []
    for shift in (0, 1):
        where = [jax.random.randint(jax.random.fold_in(key, axis), (), 0, length) for axis, length in enumerate(values.shape)]
        where[longest] = (where[longest] + shift) % values.shape[longest]
        spots.append(tuple(where))
    return values.at[spots[0]].set(low).at[spots[1]].set(high)


def levels(key, shape, shards, low, top_value):
    gain, own = 1.0, jax.random.fold_in(key, 6)
    for axis_at, shards_of in shards:
        steps = jnp.exp(jax.random.uniform(jax.random.fold_in(own, axis_at), (shards_of,), jnp.float32, low / len(shards), top_value / len(shards)))
        gain = gain * jnp.repeat(steps, shape[axis_at] // shards_of).reshape([-1 if axis == axis_at else 1 for axis in range(len(shape))])
    return gain


def ranked_wide(key, extent, count, slope):
    weights = [min(1 << octave, count + 1 - (1 << octave)) * (1 << 20) // math.isqrt((1 << octave) ** slope) + 1 for octave in range((count + 1).bit_length()) if 1 << octave <= count]
    scale = 1 + sum(weights) // (1 << 30)
    listing = np.cumsum(np.array([max(1, weight // scale) for weight in weights]))
    ticket = jax.random.randint(jax.random.fold_in(key, 1), extent, 0, int(listing[len(weights) - 1]))
    start = jnp.left_shift(1, jnp.searchsorted(jnp.asarray(listing, jnp.int32), ticket, side="right").astype(jnp.int32))
    rank = start - 1 + jax.random.randint(jax.random.fold_in(key, 4), extent, 0, 1 << 30) % jnp.minimum(start, count + 1 - start)
    return jax.random.permutation(jax.random.fold_in(key, 2), count)[rank].astype(jnp.int32)


def centred(key, shape, deviation, reach, pieces=(), kind=jnp.bfloat16):
    result = deviation * jax.random.normal(key, shape, jnp.float32)
    if pieces:
        result = result * levels(key, shape, pieces, -0.22, 0.18)
    return jnp.clip(result, -reach, reach).astype(kind)


def setup_inputs(seed: int = 0) -> dict:
    arg_keys = jax.random.split(jax.random.key(seed), 10)
    return {
        "hidden_current": draw_hidden_current(jax.random.fold_in(arg_keys[9], 71), 0),
        "hidden_proximal": draw_hidden_proximal(jax.random.fold_in(arg_keys[9], 71), 0),
        "head_current": draw_head_current(jax.random.fold_in(arg_keys[9], 71), 0),
        "head_proximal": draw_head_proximal(jax.random.fold_in(arg_keys[9], 71), 0),
        "targets": touch_ends(ranked_wide(arg_keys[4], (TOKENS,), VOCAB, 2), jax.random.fold_in(arg_keys[4], 3), 0, VOCAB - 1).astype(jnp.int32),
        "loss_mask": draw_loss_mask(jax.random.fold_in(arg_keys[9], 71), 0),
        "lengths": touch_ends(jax.random.randint(arg_keys[6], (SEQS,), 1, POSITIONS + 1), jax.random.fold_in(arg_keys[6], 1), 1, POSITIONS).astype(jnp.int32),
        "behavior_logprob": jnp.clip(-14.0 + 4.0 * jax.random.uniform(arg_keys[7], (TOKENS,), jnp.float32) ** levels(arg_keys[7], (TOKENS,), ((0, 32),), -0.2, 0.2), -14.0, -10.0),
        "advantages": centred(arg_keys[8], (TOKENS,), 1.0, 6.0, ((0, 32),), jnp.float32),
    }


CLIP_EPS = 0.2
WEIGHT_CAP = 5.0


def column_stats(logits, wanted, first_col, with_entropy):
    peak = jnp.max(logits, axis=1)
    weights = jnp.exp(logits - peak[:, None])
    total = jnp.sum(weights, axis=1)
    columns = first_col + lax.broadcasted_iota(jnp.int32, logits.shape, 1)
    picked = jnp.sum(jnp.where(columns == wanted[:, None], logits, jnp.float32(0.0)), axis=1)
    if with_entropy:
        moment = jnp.sum(weights * logits, axis=1)
        return [peak, total, moment, picked]
    return [peak, total, picked]


def token_terms(logp_current, logp_proximal, entropy, advantages, behavior, live):
    ratio = jnp.exp(logp_current - logp_proximal)
    clipped = jnp.clip(ratio, 1.0 - CLIP_EPS, 1.0 + CLIP_EPS)
    surrogate = jnp.maximum(-advantages * ratio, -advantages * clipped)
    weight = jnp.minimum(jnp.exp(logp_proximal - behavior), WEIGHT_CAP)
    return surrogate * weight * live, weight * live, entropy * live


def reference(hidden_current, hidden_proximal, head_current, head_proximal, targets, loss_mask, lengths, behavior_logprob, advantages):
    blocks = 16
    width = VOCAB // blocks

    def one_block(index):
        first_col = (index * width).astype(jnp.int32)
        part_c = lax.dynamic_slice_in_dim(head_current, first_col, width, 1)
        part_p = lax.dynamic_slice_in_dim(head_proximal, first_col, width, 1)
        logits_c = jnp.dot(hidden_current, part_c, preferred_element_type=jnp.float32)
        logits_p = jnp.dot(hidden_proximal, part_p, preferred_element_type=jnp.float32)
        return tuple(column_stats(logits_c, targets, first_col, True) + column_stats(logits_p, targets, first_col, False))

    parts = lax.map(one_block, jnp.arange(blocks, dtype=jnp.int32))
    peak_c = jnp.max(parts[0], axis=0)
    scale_c = jnp.exp(parts[0] - peak_c[None, :])
    total_c = jnp.sum(parts[1] * scale_c, axis=0)
    moment_c = jnp.sum(parts[2] * scale_c, axis=0)
    picked_c = jnp.sum(parts[3], axis=0)
    peak_p = jnp.max(parts[4], axis=0)
    total_p = jnp.sum(parts[5] * jnp.exp(parts[4] - peak_p[None, :]), axis=0)
    picked_p = jnp.sum(parts[6], axis=0)
    lse_c = peak_c + jnp.log(total_c)
    logp_c = picked_c - lse_c
    entropy = lse_c - moment_c / total_c
    logp_p = picked_p - (peak_p + jnp.log(total_p))
    place = jnp.arange(TOKENS, dtype=jnp.int32) % POSITIONS
    owner = jnp.arange(TOKENS, dtype=jnp.int32) // POSITIONS
    live = ((place < lengths[owner]) & (loss_mask == 1)).astype(jnp.float32)
    loss_t, weight_t, ent_t = token_terms(logp_c, logp_p, entropy, advantages, behavior_logprob, live)
    count = jnp.sum(live)
    stats = jnp.stack([jnp.sum(loss_t) / count, jnp.sum(weight_t) / count, jnp.sum(ent_t) / count])
    return loss_t, logp_c, stats
```

```python
import functools

import jax
import jax.numpy as jnp
from jax import lax
from jax.experimental import pallas as pl
from jax.experimental.pallas import tpu as pltpu
from jax.sharding import PartitionSpec as P

POSITIONS = 8

CLIP_EPS = 0.2
WEIGHT_CAP = 5.0
AXES = ("dp", "vocab")
MESH = pl.DeviceIdType.MESH
LANES = 128
TILE = 512
BLOCK = 64
PARTS = 4
SLOTS = 6


def flip(value, mask):
    bit = 1
    out = value
    while bit <= mask:
        if mask & bit:
            out = out + bit * (1 - 2 * ((value // bit) % 2))
        bit *= 2
    return out


def kernel(
    n_dp,
    n_v,
    target_ref,
    mask_ref,
    length_ref,
    behavior_ref,
    advantage_ref,
    hid_c_ref,
    hid_p_ref,
    head_c_ref,
    head_p_ref,
    out_ref,
    slabs,
    held,
    tags,
    aux_ref,
    hid_t,
    acc,
    stat_out,
    stat_in,
    sum_out,
    sum_in,
    slab_sem,
    own_sem,
    send_sem,
    recv_sem,
    tag_send,
    tag_recv,
    stat_send,
    stat_recv,
    sum_send,
    sum_recv,
):
    dp, v = lax.axis_index("dp"), lax.axis_index("vocab")
    me = dp * n_v + v
    n_dev = n_dp * n_v
    n_q = n_dp // 2
    half = n_q * n_v
    rows, depth = hid_c_ref.shape
    cols = head_c_ref.shape[0]
    part = depth // PARTS
    padded, tokens = acc.shape
    first_col = me * cols
    heads = (head_c_ref, head_p_ref)
    hids = (hid_c_ref, hid_p_ref)
    steps = 2 * PARTS

    def device_of(slot):
        core, rest = divmod(slot, half)
        q, z = divmod(rest, n_v)
        return (flip(dp, q * 2 + core), flip(v, z))

    def slab_copy(i):
        policy, k = divmod(i, PARTS)
        return pltpu.make_async_copy(
            heads[policy].at[:, pl.ds(k * part, part)], slabs.at[i % SLOTS], slab_sem.at[i % SLOTS]
        )

    own = [pltpu.make_async_copy(hids[p], held.at[p, 0], own_sem.at[p]) for p in range(2)]
    barrier = pltpu.get_barrier_semaphore()
    for slot in range(1, n_dev):
        pl.semaphore_signal(barrier, inc=1, device_id=device_of(slot), device_id_type=MESH)
    for copy in own:
        copy.start()
    for i in range(min(SLOTS, steps)):
        slab_copy(i).start()

    lane = lax.broadcasted_iota(jnp.int32, (rows, LANES), 1)
    row = lax.broadcasted_iota(jnp.int32, (rows, LANES), 0)
    aux = jnp.zeros((rows, LANES), jnp.float32)
    for r in range(rows):
        live = jnp.where(
            r % POSITIONS < length_ref[r // POSITIONS], jnp.where(mask_ref[r] == 1, 1.0, 0.0), 0.0
        )
        values = (target_ref[r].astype(jnp.float32), advantage_ref[r], behavior_ref[r], live)
        for n, one in enumerate(values):
            aux = jnp.where((row == r) & (lane == n), one, aux)
    aux_ref[...] = aux
    own_tag = pltpu.make_async_copy(aux_ref, tags.at[0], own_sem.at[2])
    own_tag.start()
    pl.semaphore_wait(barrier, n_dev - 1)

    sent = []

    def send(src, dst, s_sem, r_sem, slot):
        copy = pltpu.make_async_remote_copy(
            src_ref=src, dst_ref=dst, send_sem=s_sem, recv_sem=r_sem,
            device_id=device_of(slot), device_id_type=MESH,
        )
        copy.start()
        sent.append(copy)
        return copy

    bits = [1 << b for b in range(n_q.bit_length() - 1)]
    arrivals = {}

    def view(i, lo, count):
        if i is None:
            return tags.at[pl.ds(lo, count)]
        policy, k = divmod(i, PARTS)
        return held.at[policy, pl.ds(lo, count), :, pl.ds(k * part, part)]

    def message(i, lo_src, lo_dst, count, number, slot):
        s_sem = tag_send.at[number] if i is None else send_sem.at[i, number]
        r_sem = tag_recv.at[number] if i is None else recv_sem.at[i, number]
        copy = send(view(i, lo_src, count), view(i, lo_dst, count), s_sem, r_sem, slot)
        arrivals[(i, number)] = copy

    def landed(i, number):
        arrivals[(i, number)].wait_recv()

    def order_of(i):
        return bits if i is None or i % 2 == 0 else bits[::-1]

    def number_of(group):
        return n_v - 1 + group - 1

    def last_dim(order, group):
        return max(k for k, m in enumerate(order) if group & m)

    def groups_of_phase(order):
        groups = sorted(range(1, n_q), key=lambda g: (last_dim(order, g), bin(g).count("1"), g))
        return groups

    def forward(i, group):
        order = order_of(i)
        start = 0 if group == 0 else last_dim(order, group) + 1
        for k in range(start, len(order)):
            other = group ^ order[k]
            message(i, group * n_v, other * n_v, n_v, number_of(other), order[k] * n_v)

    def phase(i, j):
        order = order_of(i)
        groups = groups_of_phase(order)
        if j == 0:
            for z in range(1, n_v):
                message(i, 0, z, 1, z - 1, z)
        elif j == 1:
            for z in range(1, n_v):
                landed(i, z - 1)
            forward(i, 0)
        elif j <= len(bits):
            for g in groups:
                if last_dim(order, g) == j - 2:
                    landed(i, number_of(g))
                    forward(i, g)
        elif j == len(bits) + 1:
            for g in groups:
                if last_dim(order, g) == j - 2:
                    landed(i, number_of(g))
            message(i, 0, half, half, half - 1, half)
        else:
            landed(i, half - 1)

    last = len(bits) + 2
    for copy in own + [own_tag]:
        copy.wait()
    for i in range(steps):
        phase(i, 0)
        if i == 0:
            phase(None, 0)

    def step(t):
        for i in range(steps):
            j = t - i
            if 1 <= j <= last:
                phase(i, j)
                if i == 0:
                    phase(None, j)

    neg = float(jnp.finfo(jnp.float32).min)
    if padded > cols:
        edge = cols // 8 * 8
        acc[edge:, :] = jnp.full((padded - edge, tokens), neg, jnp.float32)

    full = cols // TILE

    def compute(i):
        policy, k = divmod(i, PARTS)
        slab_copy(i).wait()
        slab = slabs.at[i % SLOTS]
        piece = held[policy, :, :, k * part:(k + 1) * part]
        hid_t[...] = piece.astype(jnp.float32).reshape(tokens, part).T.astype(jnp.bfloat16)

        def tile(lo, width):
            at = pl.ds(lo, width)
            value = jnp.dot(slab[at, :], hid_t[...], preferred_element_type=jnp.float32)
            if k:
                value = value + acc[at, :]
            acc[at, :] = value

        @pl.loop(0, full)
        def _(n):
            tile(pl.multiple_of(n * TILE, TILE), TILE)

        if cols > full * TILE:
            tile(full * TILE, cols - full * TILE)
        if i + SLOTS < steps:
            slab_copy(i + SLOTS).start()

    def softmax(with_entropy):
        blocks = padded // BLOCK
        subs = BLOCK // 8
        width = min(tokens, 256)
        results = []
        for lo in range(0, tokens, width):
            here = slice(lo, lo + width)
            wanted = tags[pl.ds(lo // rows, width // rows)].reshape(width, LANES).T[0:1, :]
            wanted = wanted.astype(jnp.int32) - first_col
            wanted = jnp.where((wanted >= 0) & (wanted < cols), wanted, -1)
            wanted = wanted - lax.broadcasted_iota(jnp.int32, (8, width), 0)

            def largest(b, peak):
                base = pl.multiple_of(b * BLOCK, BLOCK)
                block = [acc[pl.ds(base + 8 * n, 8), here] for n in range(subs)]
                while len(block) > 1:
                    block = [jnp.maximum(x, y) for x, y in zip(block[::2], block[1::2])]
                return jnp.maximum(peak, block[0])

            peak = lax.fori_loop(0, blocks, largest, jnp.full((8, width), neg, jnp.float32))
            peak = jnp.max(peak, axis=0, keepdims=True)

            def summed(b, carry):
                total, moment, picked = carry
                base = pl.multiple_of(b * BLOCK, BLOCK)
                for n in range(subs):
                    value = acc[pl.ds(base + 8 * n, 8), here]
                    weight = jnp.exp(value - peak)
                    total = total + weight
                    if with_entropy:
                        moment = moment + weight * value
                    picked = picked + jnp.where(wanted == base + 8 * n, value, 0.0)
                return total, moment, picked

            zero = jnp.zeros((8, width), jnp.float32)
            sums = lax.fori_loop(0, blocks, summed, (zero, zero, zero))
            total, moment, picked = [jnp.sum(x, axis=0, keepdims=True) for x in sums]
            results.append((peak, total, picked, moment))
        return [jnp.concatenate([r[n] for r in results], axis=1) for n in range(4)]

    for t in range(1, last):
        step(t)
    for i in range(steps):
        step(last + i)
        compute(i)
        if i == PARTS - 1:
            found = softmax(True)
        elif i == steps - 1:
            found = found + softmax(False)
    table = jnp.concatenate(found + [jnp.zeros((LANES - 8, tokens), jnp.float32)], axis=0)
    stat_out[...] = table.T

    back = []
    for slot in range(1, n_dev):
        back.append(send(
            stat_out.at[pl.ds(slot * rows, rows)], stat_in.at[slot],
            stat_send.at[slot], stat_recv.at[slot], slot,
        ))
    stat_in[0] = stat_out[0:rows, :]
    for copy in back:
        copy.wait_recv()
    stats = stat_in[...]

    def column(n):
        return stats[:, :, n:n + 1]

    peak_c = jnp.max(column(0), axis=0, keepdims=True)
    peak_p = jnp.max(column(4), axis=0, keepdims=True)
    scale_c = jnp.exp(column(0) - peak_c)
    scale_p = jnp.exp(column(4) - peak_p)
    total_c = jnp.sum(column(1) * scale_c, axis=0)
    moment_c = jnp.sum(column(3) * scale_c, axis=0)
    picked_c = jnp.sum(column(2), axis=0)
    total_p = jnp.sum(column(5) * scale_p, axis=0)
    picked_p = jnp.sum(column(6), axis=0)
    lse_c = peak_c[0] + jnp.log(total_c)
    logp_c = picked_c - lse_c
    entropy = lse_c - moment_c / total_c
    logp_p = picked_p - (peak_p[0] + jnp.log(total_p))
    aux = aux_ref[...]
    advantages, behavior, live = aux[:, 1:2], aux[:, 2:3], aux[:, 3:4]
    ratio = jnp.exp(logp_c - logp_p)
    clipped = jnp.clip(ratio, 1.0 - CLIP_EPS, 1.0 + CLIP_EPS)
    surrogate = jnp.maximum(-advantages * ratio, -advantages * clipped)
    weight = jnp.minimum(jnp.exp(logp_p - behavior), WEIGHT_CAP)
    loss = surrogate * weight * live

    terms = jnp.where(lane == 2, loss, 0.0)
    terms = jnp.where(lane == 3, weight * live, terms)
    terms = jnp.where(lane == 4, entropy * live, terms)
    terms = jnp.where(lane == 5, live, terms)
    mine = jnp.sum(terms, axis=0, keepdims=True)
    sum_out[...] = mine
    sums = []
    for slot in range(1, n_dev):
        sums.append(send(sum_out, sum_in.at[me], sum_send.at[slot], sum_recv.at[slot], slot))
    sum_in[me] = mine
    for copy in sums:
        copy.wait_recv()
    whole = jnp.sum(sum_in[...], axis=0)
    count = whole[:, 5:6]
    result = whole / count
    result = jnp.where(lane == 0, loss, jnp.broadcast_to(result, (rows, LANES)))
    out_ref[...] = jnp.where(lane == 1, logp_c, result)
    for copy in sent:
        copy.wait_send()


def local(
    n_dp,
    n_v,
    hidden_current,
    hidden_proximal,
    head_current,
    head_proximal,
    targets,
    loss_mask,
    lengths,
    behavior_logprob,
    advantages,
):
    rows, depth = hidden_current.shape
    cols = head_current.shape[1]
    n_dev = n_dp * n_v
    tokens = n_dev * rows
    padded = -(-cols // BLOCK) * BLOCK
    messages = n_dev // 2
    vmem = pl.BlockSpec(memory_space=pltpu.VMEM)
    smem = pl.BlockSpec(memory_space=pltpu.SMEM)
    anywhere = pl.BlockSpec(memory_space=pl.ANY)
    dma = pltpu.SemaphoreType.DMA
    out = pl.pallas_call(
        functools.partial(kernel, n_dp, n_v),
        out_shape=jax.ShapeDtypeStruct((rows, LANES), jnp.float32),
        in_specs=[smem] * 5 + [anywhere, anywhere, anywhere, anywhere],
        out_specs=vmem,
        scratch_shapes=[
            pltpu.VMEM((SLOTS, cols, depth // PARTS), jnp.bfloat16),
            pltpu.VMEM((2, n_dev, rows, depth), jnp.bfloat16),
            pltpu.VMEM((n_dev, rows, LANES), jnp.float32),
            pltpu.VMEM((rows, LANES), jnp.float32),
            pltpu.VMEM((depth // PARTS, tokens), jnp.bfloat16),
            pltpu.VMEM((padded, tokens), jnp.float32),
            pltpu.VMEM((tokens, LANES), jnp.float32),
            pltpu.VMEM((n_dev, rows, LANES), jnp.float32),
            pltpu.VMEM((1, LANES), jnp.float32),
            pltpu.VMEM((n_dev, 1, LANES), jnp.float32),
            dma((SLOTS,)),
            dma((3,)),
            dma((2 * PARTS, messages)),
            dma((2 * PARTS, messages)),
            dma((messages,)),
            dma((messages,)),
            dma((n_dev,)),
            dma((n_dev,)),
            dma((n_dev,)),
            dma((n_dev,)),
        ],
        compiler_params=pltpu.CompilerParams(
            collective_id=0, has_side_effects=True, vmem_limit_bytes=67043328
        ),
    )(
        targets, loss_mask, lengths, behavior_logprob, advantages,
        hidden_current, hidden_proximal, head_current.T, head_proximal.T,
    )
    return (out[:, 0], out[:, 1], out[0, 2:5])


def solution(mesh):
    placed = (
        P(AXES, None),
        P(AXES, None),
        P(None, AXES),
        P(None, AXES),
        P(AXES),
        P(AXES),
        P(AXES),
        P(AXES),
        P(AXES),
    )
    return jax.shard_map(
        functools.partial(local, mesh.shape["dp"], mesh.shape["vocab"]),
        mesh=mesh,
        in_specs=placed,
        out_specs=(P(AXES), P(AXES), P()),
        check_vma=False,
    )
```

```python
import functools

import jax
import jax.numpy as jnp
from jax import lax
from jax.experimental import pallas as pl
from jax.experimental.pallas import tpu as pltpu
from jax.sharding import PartitionSpec as P

POSITIONS = 8

CLIP_EPS = 0.2
WEIGHT_CAP = 5.0
AXES = ("dp", "vocab")
MESH = pl.DeviceIdType.MESH
LANES = 128
TILE = 1024
BLOCK = 64
PARTS = 4
SLOTS = 6
STRIDE = 2


def flip(value, mask):
    bit = 1
    out = value
    while bit <= mask:
        if mask & bit:
            out = out + bit * (1 - 2 * ((value // bit) % 2))
        bit *= 2
    return out


def kernel(
    n_dp,
    n_v,
    target_ref,
    mask_ref,
    length_ref,
    behavior_ref,
    advantage_ref,
    hid_c_ref,
    hid_p_ref,
    head_c_ref,
    head_p_ref,
    out_ref,
    slabs,
    held,
    tags,
    aux_ref,
    hid_t,
    acc,
    stat_out,
    stat_in,
    sum_out,
    sum_in,
    slab_sem,
    own_sem,
    send_sem,
    recv_sem,
    tag_send,
    tag_recv,
    stat_send,
    stat_recv,
    sum_send,
    sum_recv,
):
    dp, v = lax.axis_index("dp"), lax.axis_index("vocab")
    me = dp * n_v + v
    n_dev = n_dp * n_v
    n_q = n_dp // 2
    half = n_q * n_v
    rows, depth = hid_c_ref.shape
    cols = head_c_ref.shape[0]
    part = depth // PARTS
    padded, tokens = acc.shape
    first_col = me * cols
    heads = (head_c_ref, head_p_ref)
    hids = (hid_c_ref, hid_p_ref)
    steps = 2 * PARTS

    def device_of(slot):
        core, rest = divmod(slot, half)
        q, z = divmod(rest, n_v)
        return (flip(dp, q * 2 + core), flip(v, z))

    def slab_copy(i):
        policy, k = divmod(i, PARTS)
        return pltpu.make_async_copy(
            heads[policy].at[:, pl.ds(k * part, part)], slabs.at[i % SLOTS], slab_sem.at[i % SLOTS]
        )

    own = [
        pltpu.make_async_copy(
            hids[p].at[:, pl.ds(k * part, part)], held.at[p, k, 0], own_sem.at[p * PARTS + k]
        )
        for p in range(2)
        for k in range(PARTS)
    ]
    barrier = pltpu.get_barrier_semaphore()
    for slot in range(1, n_dev):
        pl.semaphore_signal(barrier, inc=1, device_id=device_of(slot), device_id_type=MESH)
    for copy in own:
        copy.start()
    for i in range(min(SLOTS, steps)):
        slab_copy(i).start()

    lane = lax.broadcasted_iota(jnp.int32, (rows, LANES), 1)
    row = lax.broadcasted_iota(jnp.int32, (rows, LANES), 0)
    aux = jnp.zeros((rows, LANES), jnp.float32)
    for r in range(rows):
        live = jnp.where(
            r % POSITIONS < length_ref[r // POSITIONS], jnp.where(mask_ref[r] == 1, 1.0, 0.0), 0.0
        )
        values = (target_ref[r].astype(jnp.float32), advantage_ref[r], behavior_ref[r], live)
        for n, one in enumerate(values):
            aux = jnp.where((row == r) & (lane == n), one, aux)
    aux_ref[...] = aux
    own_tag = pltpu.make_async_copy(aux_ref, tags.at[0], own_sem.at[steps])
    own_tag.start()
    pl.semaphore_wait(barrier, n_dev - 1)

    sent = []

    def send(src, dst, s_sem, r_sem, slot):
        copy = pltpu.make_async_remote_copy(
            src_ref=src, dst_ref=dst, send_sem=s_sem, recv_sem=r_sem,
            device_id=device_of(slot), device_id_type=MESH,
        )
        copy.start()
        sent.append(copy)
        return copy

    bits = [1 << b for b in range(n_q.bit_length() - 1)]
    arrivals = {}

    def view(i, lo, count):
        if i is None:
            return tags.at[pl.ds(lo, count)]
        policy, k = divmod(i, PARTS)
        return held.at[policy, k, pl.ds(lo, count)]

    def message(i, lo_src, lo_dst, count, number, slot):
        s_sem = tag_send.at[number] if i is None else send_sem.at[i, number]
        r_sem = tag_recv.at[number] if i is None else recv_sem.at[i, number]
        copy = send(view(i, lo_src, count), view(i, lo_dst, count), s_sem, r_sem, slot)
        arrivals[(i, number)] = copy

    def landed(i, number):
        arrivals[(i, number)].wait_recv()

    def order_of(i):
        return bits if i is None or i % 2 == 0 else bits[::-1]

    def number_of(group):
        return n_v - 1 + group - 1

    def last_dim(order, group):
        return max(k for k, m in enumerate(order) if group & m)

    def groups_of_phase(order):
        groups = sorted(range(1, n_q), key=lambda g: (last_dim(order, g), bin(g).count("1"), g))
        return groups

    def forward(i, group):
        order = order_of(i)
        start = 0 if group == 0 else last_dim(order, group) + 1
        for k in range(start, len(order)):
            other = group ^ order[k]
            message(i, group * n_v, other * n_v, n_v, number_of(other), order[k] * n_v)

    def phase(i, j):
        order = order_of(i)
        groups = groups_of_phase(order)
        if j == 0:
            for z in range(1, n_v):
                message(i, 0, z, 1, z - 1, z)
        elif j == 1:
            for z in range(1, n_v):
                landed(i, z - 1)
            forward(i, 0)
        elif j <= len(bits):
            for g in groups:
                if last_dim(order, g) == j - 2:
                    landed(i, number_of(g))
                    forward(i, g)
        elif j == len(bits) + 1:
            for g in groups:
                if last_dim(order, g) == j - 2:
                    landed(i, number_of(g))
            message(i, 0, half, half, half - 1, half)
        else:
            landed(i, half - 1)

    last = len(bits) + 2
    for copy in own + [own_tag]:
        copy.wait()
    for i in range(steps):
        phase(i, 0)
        if i == 0:
            phase(None, 0)

    def step(t):
        for i in range(steps):
            j, rest = divmod(t - i, STRIDE)
            if rest == 0 and 1 <= j <= last:
                phase(i, j)
                if i == 0:
                    phase(None, j)

    neg = float(jnp.finfo(jnp.float32).min)
    if padded > cols:
        edge = cols // 8 * 8
        acc[edge:, :] = jnp.full((padded - edge, tokens), neg, jnp.float32)

    full = cols // TILE

    def compute(i):
        policy, k = divmod(i, PARTS)
        slab_copy(i).wait()
        slab = slabs.at[i % SLOTS]
        piece = held[policy, k]
        hid_t[...] = piece.astype(jnp.float32).reshape(tokens, part).T.astype(jnp.bfloat16)

        def tile(lo, width):
            at = pl.ds(lo, width)
            value = jnp.dot(slab[at, :], hid_t[...], preferred_element_type=jnp.float32)
            if k:
                value = value + acc[at, :]
            acc[at, :] = value

        @pl.loop(0, full)
        def _(n):
            tile(pl.multiple_of(n * TILE, TILE), TILE)

        if cols > full * TILE:
            tile(full * TILE, cols - full * TILE)
        if i + SLOTS < steps:
            slab_copy(i + SLOTS).start()

    def softmax(with_entropy):
        blocks = padded // BLOCK
        subs = BLOCK // 8
        width = min(tokens, 256)
        results = []
        for lo in range(0, tokens, width):
            here = slice(lo, lo + width)
            wanted = tags[pl.ds(lo // rows, width // rows)].reshape(width, LANES).T[0:1, :]
            wanted = wanted.astype(jnp.int32) - first_col
            wanted = jnp.where((wanted >= 0) & (wanted < cols), wanted, -1)
            wanted = wanted - lax.broadcasted_iota(jnp.int32, (8, width), 0)

            def largest(b, peak):
                base = pl.multiple_of(b * BLOCK, BLOCK)
                block = [acc[pl.ds(base + 8 * n, 8), here] for n in range(subs)]
                while len(block) > 1:
                    block = [jnp.maximum(x, y) for x, y in zip(block[::2], block[1::2])]
                return jnp.maximum(peak, block[0])

            peak = lax.fori_loop(0, blocks, largest, jnp.full((8, width), neg, jnp.float32))
            peak = jnp.max(peak, axis=0, keepdims=True)

            def summed(b, carry):
                total, moment, picked = carry
                base = pl.multiple_of(b * BLOCK, BLOCK)
                for n in range(subs):
                    value = acc[pl.ds(base + 8 * n, 8), here]
                    weight = jnp.exp(value - peak)
                    total = total + weight
                    if with_entropy:
                        moment = moment + weight * value
                    picked = picked + jnp.where(wanted == base + 8 * n, value, 0.0)
                return total, moment, picked

            zero = jnp.zeros((8, width), jnp.float32)
            sums = lax.fori_loop(0, blocks, summed, (zero, zero, zero))
            total, moment, picked = [jnp.sum(x, axis=0, keepdims=True) for x in sums]
            results.append((peak, total, picked, moment))
        return [jnp.concatenate([r[n] for r in results], axis=1) for n in range(4)]

    for t in range(1, STRIDE * last):
        step(t)
    for i in range(steps):
        step(STRIDE * last + i)
        compute(i)
        if i == PARTS - 1:
            found = softmax(True)
        elif i == steps - 1:
            found = found + softmax(False)
    table = jnp.concatenate(found + [jnp.zeros((LANES - 8, tokens), jnp.float32)], axis=0)
    stat_out[...] = table.T

    back = []
    for slot in range(1, n_dev):
        back.append(send(
            stat_out.at[pl.ds(slot * rows, rows)], stat_in.at[slot],
            stat_send.at[slot], stat_recv.at[slot], slot,
        ))
    stat_in[0] = stat_out[0:rows, :]
    for copy in back:
        copy.wait_recv()
    stats = stat_in[...]

    def column(n):
        return stats[:, :, n:n + 1]

    peak_c = jnp.max(column(0), axis=0, keepdims=True)
    peak_p = jnp.max(column(4), axis=0, keepdims=True)
    scale_c = jnp.exp(column(0) - peak_c)
    scale_p = jnp.exp(column(4) - peak_p)
    total_c = jnp.sum(column(1) * scale_c, axis=0)
    moment_c = jnp.sum(column(3) * scale_c, axis=0)
    picked_c = jnp.sum(column(2), axis=0)
    total_p = jnp.sum(column(5) * scale_p, axis=0)
    picked_p = jnp.sum(column(6), axis=0)
    lse_c = peak_c[0] + jnp.log(total_c)
    logp_c = picked_c - lse_c
    entropy = lse_c - moment_c / total_c
    logp_p = picked_p - (peak_p[0] + jnp.log(total_p))
    aux = aux_ref[...]
    advantages, behavior, live = aux[:, 1:2], aux[:, 2:3], aux[:, 3:4]
    ratio = jnp.exp(logp_c - logp_p)
    clipped = jnp.clip(ratio, 1.0 - CLIP_EPS, 1.0 + CLIP_EPS)
    surrogate = jnp.maximum(-advantages * ratio, -advantages * clipped)
    weight = jnp.minimum(jnp.exp(logp_p - behavior), WEIGHT_CAP)
    loss = surrogate * weight * live

    terms = jnp.where(lane == 2, loss, 0.0)
    terms = jnp.where(lane == 3, weight * live, terms)
    terms = jnp.where(lane == 4, entropy * live, terms)
    terms = jnp.where(lane == 5, live, terms)
    mine = jnp.sum(terms, axis=0, keepdims=True)
    sum_out[...] = mine
    sums = []
    for slot in range(1, n_dev):
        sums.append(send(sum_out, sum_in.at[me], sum_send.at[slot], sum_recv.at[slot], slot))
    sum_in[me] = mine
    for copy in sums:
        copy.wait_recv()
    whole = jnp.sum(sum_in[...], axis=0)
    count = whole[:, 5:6]
    result = whole / count
    result = jnp.where(lane == 0, loss, jnp.broadcast_to(result, (rows, LANES)))
    out_ref[...] = jnp.where(lane == 1, logp_c, result)
    for copy in sent:
        copy.wait_send()


def local(
    n_dp,
    n_v,
    hidden_current,
    hidden_proximal,
    head_current,
    head_proximal,
    targets,
    loss_mask,
    lengths,
    behavior_logprob,
    advantages,
):
    rows, depth = hidden_current.shape
    cols = head_current.shape[1]
    n_dev = n_dp * n_v
    tokens = n_dev * rows
    padded = -(-cols // BLOCK) * BLOCK
    messages = n_dev // 2
    vmem = pl.BlockSpec(memory_space=pltpu.VMEM)
    smem = pl.BlockSpec(memory_space=pltpu.SMEM)
    anywhere = pl.BlockSpec(memory_space=pl.ANY)
    dma = pltpu.SemaphoreType.DMA
    out = pl.pallas_call(
        functools.partial(kernel, n_dp, n_v),
        out_shape=jax.ShapeDtypeStruct((rows, LANES), jnp.float32),
        in_specs=[smem] * 5 + [anywhere, anywhere, anywhere, anywhere],
        out_specs=vmem,
        scratch_shapes=[
            pltpu.VMEM((SLOTS, cols, depth // PARTS), jnp.bfloat16),
            pltpu.VMEM((2, PARTS, n_dev, rows, depth // PARTS), jnp.bfloat16),
            pltpu.VMEM((n_dev, rows, LANES), jnp.float32),
            pltpu.VMEM((rows, LANES), jnp.float32),
            pltpu.VMEM((depth // PARTS, tokens), jnp.bfloat16),
            pltpu.VMEM((padded, tokens), jnp.float32),
            pltpu.VMEM((tokens, LANES), jnp.float32),
            pltpu.VMEM((n_dev, rows, LANES), jnp.float32),
            pltpu.VMEM((1, LANES), jnp.float32),
            pltpu.VMEM((n_dev, 1, LANES), jnp.float32),
            dma((SLOTS,)),
            dma((2 * PARTS + 1,)),
            dma((2 * PARTS, messages)),
            dma((2 * PARTS, messages)),
            dma((messages,)),
            dma((messages,)),
            dma((n_dev,)),
            dma((n_dev,)),
            dma((n_dev,)),
            dma((n_dev,)),
        ],
        compiler_params=pltpu.CompilerParams(
            collective_id=0, has_side_effects=True, vmem_limit_bytes=67043328
        ),
    )(
        targets, loss_mask, lengths, behavior_logprob, advantages,
        hidden_current, hidden_proximal, head_current.T, head_proximal.T,
    )
    return (out[:, 0], out[:, 1], out[0, 2:5])


def solution(mesh):
    placed = (
        P(AXES, None),
        P(AXES, None),
        P(None, AXES),
        P(None, AXES),
        P(AXES),
        P(AXES),
        P(AXES),
        P(AXES),
        P(AXES),
    )
    return jax.shard_map(
        functools.partial(local, mesh.shape["dp"], mesh.shape["vocab"]),
        mesh=mesh,
        in_specs=placed,
        out_specs=(P(AXES), P(AXES), P()),
        check_vma=False,
    )
```
